128 devices in a mesh: gx: 8 (over y, core), gy: 16 (over x, z).
Axes of the slice: x: 4, y: 4, z: 4, core: 2. Of those that a mesh axis runs over, the one named last changes fastest.
Arguments:
- solute_load: bfloat16 [2048, 64, 256], P(('gx', 'gy')), may hold values from 0.099609375 to 3
- walker_displacement: float32 [2048, 3, 256], P(('gx', 'gy')), may hold values from -4 to 4
- local_kelvin: float32 [2048, 256], P(('gx', 'gy')), may hold values from 0.5 to 2
- couple_kinetic_factor: float32 [32], replicated, may hold values from 0.3 to 3
- arrhenius_onset: float32 [32], replicated, may hold values from 0.2 to 1.5
- adjacent_cell_keys: int32 [2048, 16], P(('gx', 'gy')), may hold values from 0 to 24, as said below
- downstream_zone: int32 [2048, 1], P(('gx', 'gy')), may hold values from 0 to 15; in each aligned block of 16 rows (0 to 15, 16 to 31, ...) at most 2 rows name the same one
Outputs:
- arrived: bfloat16 [4096, 64, 256], P(('gx', 'gy'))
The draws below stay inside these ranges and needn't reach their ends.
Inputs may be any that keep to these rules, and one draw needn't show every extreme that they name: `adjacent_cell_keys`: each row lists 16 different codes; code o stands for the bin o // 5 - 2 rows and o % 5 - 2 columns away, and the first entry is 12, the bin itself. `downstream_zone`: entry t hands the bin to the region with the same index along gx and index t along gy; at most 2 bins of one region name the same t.
All inputs are finite; a program needn't handle non-finite values.
Results may differ from the reference program's by a relative error of at most 0.0035.
Values may be sent and summed in bfloat16 or wider, within the bound.
A program may use at most 128 MiB of HBM per device.

```python
import math
from functools import partial
import jax
import jax.numpy as jnp
import numpy as np
from jax import lax

BX = 4
BY = 4
CELL_WALKERS = 256
SPECIES = 64
NBR = 16
STEPS = 2
HALF = 32
REG_Y = 16
CELL_COUNT_ALL = 2048
CAP = 2
N_GX = 8
N_GY = 16
DEVICES = 128


def draw_adjacent_cell_keys(key, part):
    row_count = BX * BY * DEVICES
    scores = jax.random.randint(key, (row_count, 24), 0, 1 << 20) * 32 + jnp.arange(24, dtype=jnp.int32)[None, :]
    picked = jnp.argsort(scores, axis=1)[:, :NBR - 1].astype(jnp.int32)
    others = jnp.where(picked >= 12, picked + 1, picked)
    selfcode = jnp.full((row_count, 1), 12, jnp.int32)
    return jnp.concatenate([selfcode, others], axis=1).astype(jnp.int32)


def level_of(key, shape, pieces, smallest, largest):
    def one(axis_at, blocks):
        steps = jax.random.uniform(jax.random.fold_in(jax.random.fold_in(key, 6), axis_at), (blocks,), jnp.float32, smallest / len(pieces), largest / len(pieces))
        return jnp.repeat(jnp.exp(steps), shape[axis_at] // blocks).reshape((-1,) + (1,) * (len(shape) - axis_at - 1))

    level = one(*pieces[0])
    for cut in pieces[1:]:
        level = level * one(*cut)
    return level


def routed_block(stream_key, own, number, rows, number_of, top, bound, lean):
    ranking = jax.random.permutation(stream_key, number_of)
    heavy_load, usual = shares(number_of, rows * top, bound, lean, True), shares(number_of, rows * top, bound, lean, False)
    places = jnp.arange(number_of)

    def named(lengths, offset_by):
        used = int((lengths > 0).sum())
        fixed = max(1, used // 4)
        shifted = fixed + (places - fixed + offset_by * (used - fixed)) % max(1, number_of - fixed)
        return jnp.zeros((number_of,), jnp.int32).at[ranking[jnp.where(places < fixed, places, shifted)]].set(jnp.asarray(lengths, jnp.int32))

    lengths = jnp.where(number % 4 == 0, named(heavy_load, number // 4), named(usual, number - number // 4 - 1))
    mixed = jax.random.permutation(jax.random.fold_in(own, 3), number_of)
    source_of, taker = mixed[0:number_of // 2 * 2:2], mixed[1:number_of // 2 * 2:2]
    room = jnp.minimum(lengths[source_of] - 1, bound - lengths[taker]) // 2
    room = jnp.where((source_of == ranking[0]) | (taker == ranking[0]) | (lengths[taker] == 0), 0, jnp.maximum(room, 0))
    shifted = jax.random.randint(jax.random.fold_in(own, 4), (number_of // 2,), 0, 1 << 20) % (room + 1)
    lengths = lengths.at[source_of].add(-shifted).at[taker].add(shifted)
    members = jnp.searchsorted(jnp.cumsum(lengths), jnp.arange(rows * top), side="right").astype(jnp.int32)
    grid = members.reshape(top, rows).T
    grid = grid[jax.random.permutation(jax.random.fold_in(own, 1), rows)]
    offset_by = jax.random.randint(jax.random.fold_in(own, 2), (rows, 1), 0, top)
    return jnp.take_along_axis(grid, (jnp.arange(top)[None, :] + offset_by) % top, axis=1)


def shares(amount, total, reach, lean, full):
    weights = [(1 << 20) // math.isqrt(standing ** lean) + 1 for standing in range(1, amount + 1)]
    largest = reach if full else min(reach, max(-(-total // amount), total * weights[0] // sum(weights)))
    least = 1 if total - largest >= amount - 1 else 0
    holding, surplus = [largest] + [least] * (amount - 1), total - largest - least * (amount - 1)
    while surplus > 0:
        free = [i for i in range(1, amount) if holding[i] < largest] or [i for i in range(1, amount) if holding[i] < reach]
        pool, budget = sum([weights[i] for i in free]), surplus
        for i in free:
            addition = min(reach - holding[i], max(1, budget * weights[i] // pool), surplus)
            holding[i] = holding[i] + addition
            surplus = surplus - addition
    return np.array(holding)


def bell_draw(rng, dims, width, most, cuts=(), kind=jnp.bfloat16):
    values = jax.random.normal(rng, dims, jnp.float32) * width
    if len(cuts) > 0:
        values = level_of(rng, dims, cuts, -0.22, 0.18) * values
    return jnp.clip(values, min=-most, max=most).astype(kind)


def setup_inputs(seed: int = 0) -> dict:
    key_list = jax.random.split(jax.random.key(seed), 8)
    solute_load = jnp.clip(jnp.exp(math.log(3.0) - 3.4051113 * jax.random.uniform(key_list[0], (CELL_COUNT_ALL, SPECIES, CELL_WALKERS), jnp.float32) ** level_of(key_list[0], (CELL_COUNT_ALL, SPECIES, CELL_WALKERS), ((0, 128),), -0.2, 0.2)), 0.099609375, 3.0).astype(jnp.bfloat16)
    walker_displacement = bell_draw(key_list[1], (CELL_COUNT_ALL, 3, CELL_WALKERS), 0.8, 4.0, ((0, 128),), jnp.float32)
    local_kelvin = jnp.clip(0.5 + 1.5 * jax.random.uniform(key_list[2], (CELL_COUNT_ALL, CELL_WALKERS), jnp.float32) ** level_of(key_list[2], (CELL_COUNT_ALL, CELL_WALKERS), ((0, 128),), -0.2, 0.2), 0.5, 2.0)
    couple_kinetic_factor = jnp.clip(jnp.exp(jax.random.uniform(key_list[3], (HALF,), jnp.float32, math.log(0.3), math.log(3.0))), 0.3, 3.0)
    arrhenius_onset = jnp.clip(jax.random.uniform(key_list[4], (HALF,), jnp.float32, 0.2, 1.5), 0.2, 1.5)
    adjacent_cell_keys = draw_adjacent_cell_keys(jax.random.fold_in(key_list[7], 71), 0)
    downstream_zone_keys = jax.random.split(jax.random.fold_in(key_list[6], 1), CELL_COUNT_ALL // (BX * BY))
    downstream_zone_turns = jax.random.permutation(jax.random.fold_in(key_list[6], 3), CELL_COUNT_ALL // (BX * BY))
    downstream_zone = jax.vmap(lambda own, number: routed_block(jax.random.fold_in(key_list[6], 2), own, number, BX * BY, REG_Y, 1, CAP, 2))(downstream_zone_keys, downstream_zone_turns).reshape((CELL_COUNT_ALL, 1))
    return dict(solute_load=solute_load, walker_displacement=walker_displacement, local_kelvin=local_kelvin, couple_kinetic_factor=couple_kinetic_factor, arrhenius_onset=arrhenius_onset, adjacent_cell_keys=adjacent_cell_keys, downstream_zone=downstream_zone)


inverse_width = 4.0


def mesh_sequence(flat_rows):
    trailing = flat_rows.shape[1:]
    shaped = flat_rows.reshape((N_GX, N_GY, BX, BY) + trailing)
    permuted_axes = (0, 2, 1, 3) + tuple(range(4, 4 + len(trailing)))
    return shaped.transpose(permuted_axes).reshape((N_GX * BX, N_GY * BY) + trailing)


def device_order(mesh_vertical):
    trailing = mesh_vertical.shape[2:]
    shaped = mesh_vertical.reshape((N_GX, BX, N_GY, BY) + trailing)
    permuted_axes = (0, 2, 1, 3) + tuple(range(4, 4 + len(trailing)))
    return shaped.transpose(permuted_axes).reshape((-1,) + trailing)


def react(mixture, warming_curve, couple_kinetic_factor, arrhenius_onset):
    halves = mixture.shape[1] // 2
    kind_one = mixture[:, :halves]
    kind_two = mixture[:, halves:]
    speeds = couple_kinetic_factor[None, :, None] * jnp.exp(-arrhenius_onset[None, :, None] / warming_curve[:, None, :])
    reacted = speeds * kind_one * kind_two / (1.0 + speeds * (kind_one + kind_two))
    return jnp.concatenate([kind_one - reacted, kind_two - reacted], axis=1).astype(jnp.bfloat16)


def mix_group(ext_species, ext_pos, couple_kinetic_factor, arrhenius_onset, packet):
    centre, neighbour_idx, offsets, inside, warming_curve = packet
    centre_pos = ext_pos[centre]
    neigh_pos = ext_pos[neighbour_idx]
    shift_along = (offsets // 5 - 2).astype(jnp.float32)
    shift_across = (offsets % 5 - 2).astype(jnp.float32)
    offset_gap = centre_pos[:, None, 0, :, None] - neigh_pos[:, :, 0, None, :] - shift_along[:, :, None, None]
    squared = offset_gap * offset_gap
    offset_gap = centre_pos[:, None, 1, :, None] - neigh_pos[:, :, 1, None, :] - shift_across[:, :, None, None]
    squared = squared + offset_gap * offset_gap
    offset_gap = centre_pos[:, None, 2, :, None] - neigh_pos[:, :, 2, None, :]
    squared = squared + offset_gap * offset_gap
    kernel = jnp.exp(-squared * inverse_width) * inside[:, :, None, None]
    row_total = jnp.sum(kernel, axis=(1, 3))
    weights = (kernel / row_total[:, None, :, None]).astype(jnp.bfloat16)
    sources = ext_species[neighbour_idx]
    mixture = jnp.einsum('gksq,gkpq->gsp', sources.astype(jnp.float32), weights.astype(jnp.float32))
    return react(mixture, warming_curve, couple_kinetic_factor, arrhenius_onset)


def reference(solute_load, walker_displacement, local_kelvin, couple_kinetic_factor, arrhenius_onset, adjacent_cell_keys, downstream_zone):
    mesh_vertical = N_GX * BX
    mesh_horizontal = N_GY * BY
    species_grid = mesh_sequence(solute_load)
    pos_grid = mesh_sequence(walker_displacement)
    warming_curve = mesh_sequence(local_kelvin).reshape(mesh_vertical * mesh_horizontal, CELL_WALKERS)
    offsets_list = mesh_sequence(adjacent_cell_keys).reshape(mesh_vertical * mesh_horizontal, NBR)
    coord_x = jnp.repeat(jnp.arange(mesh_vertical, dtype=jnp.int32), mesh_horizontal)
    coord_y = jnp.tile(jnp.arange(mesh_horizontal, dtype=jnp.int32), mesh_vertical)
    row_width = mesh_horizontal + 4
    centre = (coord_x + 2) * row_width + coord_y + 2
    target_x = coord_x[:, None] + offsets_list // 5 - 2
    target_y = coord_y[:, None] + offsets_list % 5 - 2
    neighbour_idx = (target_x + 2) * row_width + target_y + 2
    inside = ((target_x >= 0) & (target_x < mesh_vertical) & (target_y >= 0) & (target_y < mesh_horizontal)).astype(jnp.float32)
    padded_pos = jnp.pad(pos_grid, ((2, 2), (2, 2), (0, 0), (0, 0))).reshape(-1, 3, CELL_WALKERS)
    packets = tuple(member.reshape((-1, 16) + member.shape[1:]) for member in (centre, neighbour_idx, offsets_list, inside, warming_curve))
    for repeat in range(STEPS):
        padded = jnp.pad(species_grid, ((2, 2), (2, 2), (0, 0), (0, 0))).reshape(-1, SPECIES, CELL_WALKERS)
        result = lax.map(partial(mix_group, padded, padded_pos, couple_kinetic_factor, arrhenius_onset), packets)
        species_grid = result.reshape(mesh_vertical, mesh_horizontal, SPECIES, CELL_WALKERS)
    finished = device_order(species_grid)
    target = downstream_zone[:, 0].reshape(N_GX, N_GY, BX * BY)
    chosen = (target[..., None] == jnp.arange(N_GY, dtype=jnp.int32)).astype(jnp.int32)
    earlier_count = jnp.cumsum(chosen, axis=2) - chosen
    order_slot = jnp.sum(earlier_count * chosen, axis=3)
    band_ids = jnp.arange(N_GX, dtype=jnp.int32)[:, None, None]
    source_ids = jnp.arange(N_GY, dtype=jnp.int32)[None, :, None]
    row_index = ((band_ids * N_GY + target) * N_GY + source_ids) * CAP + order_slot
    arrived = jnp.zeros((N_GX * N_GY * N_GY * CAP, SPECIES, CELL_WALKERS), jnp.bfloat16)
    return arrived.at[row_index.reshape(-1)].set(finished)
```

```python
import functools

import jax
import jax.numpy as jnp
from jax import lax
from jax.experimental import pallas as pl
from jax.experimental.pallas import tpu as pltpu
from jax.sharding import PartitionSpec as P

BX = 4
BY = 4
NBR = 16
BINS = BX * BY
EX = BX + 4
EY = BY + 4
SHARPNESS = 4.0
FAR = -100000.0
MESH = pl.DeviceIdType.MESH
f32 = jnp.float32
bf16 = jnp.bfloat16

STEPS8 = [(0, 1), (0, -1), (1, 0), (-1, 0), (1, 1), (1, -1), (-1, 1), (-1, -1)]


def split3(x):
    x1 = x.astype(bf16).astype(f32)
    rest = x - x1
    x2 = rest.astype(bf16).astype(f32)
    x3 = (rest - x2).astype(bf16).astype(f32)
    return x1, x2, x3


def span(step, size):
    if step == 1:
        return size - 2, 2, 0
    if step == -1:
        return 0, 2, size + 2
    return 0, size, 2


def kernel(
    n_gx,
    n_gy,
    codes,
    zone,
    pos,
    kelvin,
    factor,
    onset,
    load,
    out,
    posx,
    points,
    tiles,
    totals,
    first,
    second,
    final,
    packed,
    own_sem,
    pos_send,
    pos_recv,
    load_send,
    load_recv,
    halo_send,
    halo_recv,
    hand_send,
    hand_recv,
):
    gx = lax.axis_index("gx")
    gy = lax.axis_index("gy")

    def at(dx, dy):
        return (lax.rem(gx + dx + n_gx, n_gx), lax.rem(gy + dy + n_gy, n_gy))

    barrier = pltpu.get_barrier_semaphore()
    partners = [(dx, dy) for dx, dy in STEPS8] + [(0, r) for r in range(2, n_gy - 1)]
    for dx, dy in partners:
        pl.semaphore_signal(barrier, inc=1, device_id=at(dx, dy), device_id_type=MESH)

    own_load = pltpu.make_async_copy(load, first.at[pl.ds(2, BX), pl.ds(2, BY)], own_sem.at[0])
    own_load.start()
    own_pos = pltpu.make_async_copy(pos, posx.at[pl.ds(2, BX), pl.ds(2, BY)], own_sem.at[1])
    own_pos.start()

    eye = lax.broadcasted_iota(jnp.int32, (32, 32), 0) == lax.broadcasted_iota(
        jnp.int32, (32, 32), 1
    )

    def column(ref):
        return jnp.sum(jnp.where(eye, ref[...], 0.0), axis=1, keepdims=True)

    factors = column(factor)
    onsets = column(onset)

    pl.semaphore_wait(barrier, len(partners))

    def swap(source, framed, send, recv):
        copies = []
        for number, (dx, dy) in enumerate(STEPS8):
            row, rows, to_row = span(dx, BX)
            col, cols, to_col = span(dy, BY)
            copies.append(
                pltpu.make_async_remote_copy(
                    src_ref=source.at[pl.ds(row, rows), pl.ds(col, cols)],
                    dst_ref=framed.at[pl.ds(to_row, rows), pl.ds(to_col, cols)],
                    send_sem=send.at[number],
                    recv_sem=recv.at[number],
                    device_id=at(dx, dy),
                    device_id_type=MESH,
                )
            )
        for copy in copies:
            copy.start()
        return copies

    pos_copies = swap(pos, posx, pos_send, pos_recv)
    load_copies = swap(load, first, load_send, load_recv)

    own_pos.wait()
    for copy in pos_copies:
        copy.wait_recv()

    row8 = lax.broadcasted_iota(jnp.int32, (8, 256), 0)
    none = jnp.zeros((5, 256), f32)

    def point_rows(x, y):
        where = jnp.concatenate([posx[x, y], none], axis=0)
        norm = -SHARPNESS * jnp.sum(where * where, axis=0, keepdims=True)
        rows = jnp.where(row8 == 3, 1.0, jnp.where(row8 == 4, norm, where))
        p1, p2, p3 = split3(rows)
        return jnp.concatenate([p1, p2, p1, p2, p3, p1, jnp.zeros((16, 256), f32)], axis=0)

    def prepare(x, carry):
        for y in range(EY // 2):
            rows = jnp.concatenate([point_rows(x, 2 * y), point_rows(x, 2 * y + 1)], axis=0)
            points[x * (EY // 2) + y] = rows.T.astype(bf16)
        return carry

    lax.fori_loop(0, EX, prepare, 0)

    def neighbour(b, k):
        code = codes[b, k]
        along = ((code * 13) >> 6) - 2
        across = code - (along + 2) * 5 - 2
        inside_x = gx * BX + b // BY + along
        inside_y = gy * BY + b % BY + across
        inside = (
            (inside_x >= 0)
            & (inside_x < n_gx * BX)
            & (inside_y >= 0)
            & (inside_y < n_gy * BY)
        )
        return along, across, inside

    def weigh(b, carry):
        own = jnp.concatenate([pos[b // BY, b % BY], none], axis=0)
        total = jnp.zeros((8, 256), f32)
        for k in range(NBR):
            along, across, inside = neighbour(b, k)
            place = (b // BY + 2 + along) * EY + b % BY + 2 + across
            odd = (place & 1).astype(f32)
            shift = jnp.where(
                row8 == 0, along.astype(f32), jnp.where(row8 == 1, across.astype(f32), 0.0)
            )
            there = own - shift
            norm = -SHARPNESS * jnp.sum(there * there, axis=0, keepdims=True)
            norm = norm + jnp.where(inside, 0.0, FAR)
            rows = jnp.where(
                row8 == 3, norm, jnp.where(row8 == 4, 1.0, there * (2.0 * SHARPNESS))
            )
            p1, p2, p3 = split3(rows)
            rows = jnp.concatenate(
                [p1, p1, p2, p2, p1, p3, jnp.zeros((16, 256), f32)], axis=0
            ).astype(bf16)
            rows = jnp.concatenate(
                [rows * (1.0 - odd).astype(bf16), rows * odd.astype(bf16)], axis=0
            )
            power = jnp.dot(points[place >> 1], rows, preferred_element_type=f32)
            tile = jnp.exp(power)
            total = total + jnp.sum(tile.reshape(32, 8, 256), axis=0)
            tiles[b * NBR + k] = tile.astype(bf16)
        totals[b] = total
        return carry

    lax.fori_loop(0, BINS, weigh, 0)

    def mix(framed, b):
        sources = []
        for k in range(NBR):
            along, across, _ = neighbour(b, k)
            sources.append(framed[b // BY + 2 + along, b % BY + 2 + across])
        sources = jnp.concatenate(sources, axis=1)
        weights = tiles[pl.ds(b * NBR, NBR)].reshape(NBR * 256, 256)
        mixture = jnp.dot(sources, weights, preferred_element_type=f32)
        mixture = mixture / jnp.sum(totals[b], axis=0, keepdims=True)
        speed = factors * jnp.exp(-onsets / kelvin[pl.ds(b, 1)])
        u = mixture[:32]
        v = mixture[32:]
        reacted = speed * u * v / (1.0 + speed * (u + v))
        return jnp.concatenate([u - reacted, v - reacted], axis=0).astype(bf16)

    own_load.wait()
    for copy in load_copies:
        copy.wait_recv()

    def halo(b):
        i = b // BY
        j = b % BY
        dx = (i // 2) * 2 - 1
        dy = (j // 2) * 2 - 1
        return [
            pltpu.make_async_remote_copy(
                src_ref=second.at[i + 2, j + 2],
                dst_ref=second.at[i + 2 - BX * sx, j + 2 - BY * sy],
                send_sem=halo_send.at[kind, b],
                recv_sem=halo_recv.at[kind, b],
                device_id=at(sx, sy),
                device_id_type=MESH,
            )
            for kind, (sx, sy) in enumerate([(0, dy), (dx, dy), (dx, 0)])
        ]

    def send(b):
        for copy in halo(b):
            copy.start()

    second[2, 2] = mix(first, 0)

    def step_one(b, carry):
        second[b // BY + 2, b % BY + 2] = mix(first, b)
        send(b - 1)
        return carry

    lax.fori_loop(1, BINS, step_one, 0)
    send(BINS - 1)

    def arrive(b, carry):
        for copy in halo(b):
            copy.wait_recv()
        return carry

    lax.fori_loop(0, BINS, arrive, 0)

    def step_two(b, carry):
        final[b] = mix(second, b)
        return carry

    lax.fori_loop(0, BINS, step_two, 0)

    def pack(t):
        found = [jnp.int32(0), jnp.int32(0)]
        count = jnp.int32(0)
        for b in range(BINS):
            hit = zone[b, 0] == t
            found[0] = jnp.where(hit & (count == 0), b, found[0])
            found[1] = jnp.where(hit & (count == 1), b, found[1])
            count = count + hit.astype(jnp.int32)
        for c in range(2):
            keep = (count > c).astype(f32).astype(bf16)
            packed[2 * t + c] = final[found[c]] * keep

    def give(r):
        to = lax.rem(gy + r, n_gy)
        return pltpu.make_async_remote_copy(
            src_ref=packed.at[pl.ds(2 * to, 2)],
            dst_ref=out.at[pl.ds(2 * gy, 2)],
            send_sem=hand_send.at[r],
            recv_sem=hand_recv.at[r],
            device_id=(gx, to),
            device_id_type=MESH,
        )

    def pack_at(r, carry):
        pack(lax.rem(gy + r, n_gy))
        return carry

    lax.fori_loop(1, n_gy, pack_at, 0)

    def hand_over(r, carry):
        give(r).start()
        return carry

    lax.fori_loop(1, n_gy, hand_over, 0)
    pack(gy)
    stay = pltpu.make_async_copy(
        packed.at[pl.ds(2 * gy, 2)], out.at[pl.ds(2 * gy, 2)], own_sem.at[2]
    )
    stay.start()

    for copy in pos_copies + load_copies:
        copy.wait_send()

    def sent(b, carry):
        for copy in halo(b):
            copy.wait_send()
        return carry

    lax.fori_loop(0, BINS, sent, 0)

    def taken(r, carry):
        give(r).wait()
        return carry

    lax.fori_loop(1, n_gy, taken, 0)
    stay.wait()


def body(n_gx, n_gy, load, pos, kelvin, factor, onset, codes, zone):
    species, walkers = load.shape[1:]
    smem = pl.BlockSpec(memory_space=pltpu.SMEM)
    vmem = pl.BlockSpec(memory_space=pltpu.VMEM)
    anywhere = pl.BlockSpec(memory_space=pl.ANY)
    dma = pltpu.SemaphoreType.DMA
    return pl.pallas_call(
        functools.partial(kernel, n_gx, n_gy),
        out_shape=jax.ShapeDtypeStruct((2 * n_gy, species, walkers), bf16),
        in_specs=[smem, smem, vmem, vmem, vmem, vmem, anywhere],
        out_specs=anywhere,
        scratch_shapes=[
            pltpu.VMEM((EX, EY, 3, walkers), f32),
            pltpu.VMEM((EX * EY // 2, walkers, 128), bf16),
            pltpu.VMEM((BINS * NBR, walkers, walkers), bf16),
            pltpu.VMEM((BINS, 8, walkers), f32),
            pltpu.VMEM((EX, EY, species, walkers), bf16),
            pltpu.VMEM((EX, EY, species, walkers), bf16),
            pltpu.VMEM((BINS, species, walkers), bf16),
            pltpu.VMEM((2 * n_gy, species, walkers), bf16),
            dma((3,)),
            dma((8,)),
            dma((8,)),
            dma((8,)),
            dma((8,)),
            dma((3, BINS)),
            dma((3, BINS)),
            dma((n_gy,)),
            dma((n_gy,)),
        ],
        compiler_params=pltpu.CompilerParams(
            collective_id=0, has_side_effects=True, vmem_limit_bytes=67043328
        ),
    )(
        codes,
        zone,
        pos.reshape(BX, BY, 3, walkers),
        kelvin,
        factor.reshape(1, -1),
        onset.reshape(1, -1),
        load.reshape(BX, BY, species, walkers),
    )


def solution(mesh):
    both = ("gx", "gy")
    in_specs = (
        P(both, None, None),
        P(both, None, None),
        P(both, None),
        P(),
        P(),
        P(both, None),
        P(both, None),
    )
    return jax.shard_map(
        functools.partial(body, mesh.shape["gx"], mesh.shape["gy"]),
        mesh=mesh,
        in_specs=in_specs,
        out_specs=P(both, None, None),
        check_vma=False,
    )
```

```python
import functools

import jax
import jax.numpy as jnp
from jax import lax
from jax.experimental import pallas as pl
from jax.experimental.pallas import tpu as pltpu
from jax.sharding import PartitionSpec as P

BX = 4
BY = 4
NBR = 16
BINS = BX * BY
EX = BX + 4
EY = BY + 4
SHARPNESS = 4.0
FAR = -100000.0
MESH = pl.DeviceIdType.MESH
f32 = jnp.float32
bf16 = jnp.bfloat16

STEPS8 = [(0, 1), (0, -1), (1, 0), (-1, 0), (1, 1), (1, -1), (-1, 1), (-1, -1)]


SIDE = 4


def hops(step):
    return min(step, SIDE - step)


HANDS = sorted(
    ((ox, oz) for ox in range(SIDE) for oz in range(SIDE)),
    key=lambda step: (-hops(step[0]) - hops(step[1]), step),
)


def split3(x):
    x1 = x.astype(bf16).astype(f32)
    rest = x - x1
    x2 = rest.astype(bf16).astype(f32)
    x3 = (rest - x2).astype(bf16).astype(f32)
    return x1, x2, x3


def span(step, size):
    if step == 1:
        return size - 2, 2, 0
    if step == -1:
        return 0, 2, size + 2
    return 0, size, 2


def kernel(
    n_gx,
    n_gy,
    codes,
    zone,
    planes,
    kelvin,
    factor,
    onset,
    load,
    out,
    pos,
    posx,
    points,
    tiles,
    totals,
    first,
    second,
    final,
    packed,
    place_of,
    order,
    begin,
    amount,
    own_sem,
    pos_send,
    pos_recv,
    load_send,
    load_recv,
    halo_send,
    halo_recv,
    hand_send,
    hand_recv,
):
    gx = lax.axis_index("gx")
    gy = lax.axis_index("gy")

    def at(dx, dy):
        return (lax.rem(gx + dx + n_gx, n_gx), lax.rem(gy + dy + n_gy, n_gy))

    barrier = pltpu.get_barrier_semaphore()
    partners = [(dx, dy) for dx, dy in STEPS8] + [(0, r) for r in range(2, n_gy - 1)]
    for dx, dy in partners:
        pl.semaphore_signal(barrier, inc=1, device_id=at(dx, dy), device_id_type=MESH)

    own_load = pltpu.make_async_copy(load, first.at[pl.ds(2, BX), pl.ds(2, BY)], own_sem.at[0])
    own_load.start()
    for b in range(BINS):
        mine = jnp.concatenate([planes[c, pl.ds(b, 1)] for c in range(3)], axis=0)
        pos[b // BY, b % BY] = mine
        posx[b // BY + 2, b % BY + 2] = mine

    eye = lax.broadcasted_iota(jnp.int32, (32, 32), 0) == lax.broadcasted_iota(
        jnp.int32, (32, 32), 1
    )

    def column(ref):
        return jnp.sum(jnp.where(eye, ref[...], 0.0), axis=1, keepdims=True)

    factors = column(factor)
    onsets = column(onset)

    pl.semaphore_wait(barrier, len(partners))

    def swap(source, framed, send, recv):
        copies = []
        for number, (dx, dy) in enumerate(STEPS8):
            row, rows, to_row = span(dx, BX)
            col, cols, to_col = span(dy, BY)
            copies.append(
                pltpu.make_async_remote_copy(
                    src_ref=source.at[pl.ds(row, rows), pl.ds(col, cols)],
                    dst_ref=framed.at[pl.ds(to_row, rows), pl.ds(to_col, cols)],
                    send_sem=send.at[number],
                    recv_sem=recv.at[number],
                    device_id=at(dx, dy),
                    device_id_type=MESH,
                )
            )
        for copy in copies:
            copy.start()
        return copies

    me_x = gy // SIDE
    me_z = lax.rem(gy, SIDE)

    def target(p):
        over_x = jnp.int32(0)
        over_z = jnp.int32(0)
        for number, (ox, oz) in enumerate(HANDS):
            over_x = jnp.where(p == number, ox, over_x)
            over_z = jnp.where(p == number, oz, over_z)
        return lax.rem(me_x + over_x, SIDE) * SIDE + lax.rem(me_z + over_z, SIDE)

    pos_copies = swap(pos, posx, pos_send, pos_recv)
    load_copies = swap(load, first, load_send, load_recv)

    for number, (ox, oz) in enumerate(HANDS):
        place_of[ox * SIDE + oz] = jnp.int32(number)
    places = []
    for b in range(BINS):
        to = zone[0, b]
        over_x = ((to >> 2) - me_x) & 3
        over_z = ((to & 3) - me_z) & 3
        places.append(place_of[over_x * SIDE + over_z])
    ranks = [jnp.int32(0) for _ in range(BINS)]
    for b in range(BINS):
        for c in range(b):
            ahead = (places[c] <= places[b]).astype(jnp.int32)
            ranks[b] = ranks[b] + ahead
            ranks[c] = ranks[c] + (1 - ahead)
    for i in range(BINS):
        bin_at = jnp.int32(0)
        for b in range(BINS):
            bin_at = jnp.where(ranks[b] == i, b, bin_at)
        order[i] = bin_at
    before = jnp.int32(0)
    for p in range(n_gy):
        here = jnp.int32(0)
        for b in range(BINS):
            here = here + (places[b] == p).astype(jnp.int32)
        begin[p] = before
        amount[p] = here
        before = before + here

    for copy in pos_copies:
        copy.wait_recv()

    row8 = lax.broadcasted_iota(jnp.int32, (8, 256), 0)
    none = jnp.zeros((5, 256), f32)

    def point_rows(x, y):
        where = jnp.concatenate([posx[x, y], none], axis=0)
        norm = -SHARPNESS * jnp.sum(where * where, axis=0, keepdims=True)
        rows = jnp.where(row8 == 3, 1.0, jnp.where(row8 == 4, norm, where))
        p1, p2, p3 = split3(rows)
        return jnp.concatenate([p1, p2, p1, p2, p3, p1, jnp.zeros((16, 256), f32)], axis=0)

    def prepare(x, carry):
        for y in range(EY // 2):
            rows = jnp.concatenate([point_rows(x, 2 * y), point_rows(x, 2 * y + 1)], axis=0)
            points[x * (EY // 2) + y] = rows.T.astype(bf16)
        return carry

    lax.fori_loop(0, EX, prepare, 0)

    def neighbour(b, k):
        code = codes[b, k]
        along = ((code * 13) >> 6) - 2
        across = code - (along + 2) * 5 - 2
        inside_x = gx * BX + b // BY + along
        inside_y = gy * BY + b % BY + across
        inside = (
            (inside_x >= 0)
            & (inside_x < n_gx * BX)
            & (inside_y >= 0)
            & (inside_y < n_gy * BY)
        )
        return along, across, inside

    def weigh(b, carry):
        own = jnp.concatenate([pos[b // BY, b % BY], none], axis=0)
        total = jnp.zeros((8, 256), f32)
        for k in range(NBR):
            along, across, inside = neighbour(b, k)
            place = (b // BY + 2 + along) * EY + b % BY + 2 + across
            odd = (place & 1).astype(f32)
            shift = jnp.where(
                row8 == 0, along.astype(f32), jnp.where(row8 == 1, across.astype(f32), 0.0)
            )
            there = own - shift
            norm = -SHARPNESS * jnp.sum(there * there, axis=0, keepdims=True)
            norm = norm + jnp.where(inside, 0.0, FAR)
            rows = jnp.where(
                row8 == 3, norm, jnp.where(row8 == 4, 1.0, there * (2.0 * SHARPNESS))
            )
            p1, p2, p3 = split3(rows)
            rows = jnp.concatenate(
                [p1, p1, p2, p2, p1, p3, jnp.zeros((16, 256), f32)], axis=0
            ).astype(bf16)
            rows = jnp.concatenate(
                [rows * (1.0 - odd).astype(bf16), rows * odd.astype(bf16)], axis=0
            )
            power = jnp.dot(points[place >> 1], rows, preferred_element_type=f32)
            tile = jnp.exp(power)
            total = total + jnp.sum(tile.reshape(32, 8, 256), axis=0)
            tiles[b * NBR + k] = tile.astype(bf16)
        totals[b] = total
        return carry

    lax.fori_loop(0, BINS - BY, weigh, 0)

    def mix(framed, b):
        sources = []
        for k in range(NBR):
            along, across, _ = neighbour(b, k)
            sources.append(framed[b // BY + 2 + along, b % BY + 2 + across])
        sources = jnp.concatenate(sources, axis=1)
        weights = tiles[pl.ds(b * NBR, NBR)].reshape(NBR * 256, 256)
        mixture = jnp.dot(sources, weights, preferred_element_type=f32)
        mixture = mixture / jnp.sum(totals[b], axis=0, keepdims=True)
        speed = factors * jnp.exp(-onsets / kelvin[pl.ds(b, 1)])
        u = mixture[:32]
        v = mixture[32:]
        reacted = speed * u * v / (1.0 + speed * (u + v))
        return jnp.concatenate([u - reacted, v - reacted], axis=0).astype(bf16)

    own_load.wait()
    for copy in load_copies:
        copy.wait_recv()

    def halo(i):
        dx = (i // 2) * 2 - 1
        row = i + 2
        far = row - BX * dx
        plan = [
            (dx, -1, 2, 2, far, BY + 2),
            (dx, 1, BY, 2, far, 0),
            (0, -1, 2, 2, row, BY + 2),
            (0, 1, BY, 2, row, 0),
            (dx, 0, 2, BY, far, 2),
        ]
        return [
            pltpu.make_async_remote_copy(
                src_ref=second.at[row, pl.ds(col, cols)],
                dst_ref=second.at[to_row, pl.ds(to_col, cols)],
                send_sem=halo_send.at[kind, i],
                recv_sem=halo_recv.at[kind, i],
                device_id=at(sx, sy),
                device_id_type=MESH,
            )
            for kind, (sx, sy, col, cols, to_row, to_col) in enumerate(plan)
        ]

    def step_one(i, carry):
        for j in range(BY):
            second[i + 2, j + 2] = mix(first, i * BY + j)
        for copy in halo(i):
            copy.start()
        return carry

    lax.fori_loop(0, BX - 1, step_one, 0)
    lax.fori_loop(BINS - BY, BINS, weigh, 0)
    step_one(BX - 1, 0)

    def arrive(i, carry):
        for copy in halo(i):
            copy.wait_recv()
        return carry

    lax.fori_loop(0, BX, arrive, 0)

    def give(p):
        to = target(p)
        return pltpu.make_async_remote_copy(
            src_ref=packed.at[pl.ds(2 * p, 2)],
            dst_ref=out.at[pl.ds(2 * gy, 2)],
            send_sem=hand_send.at[p],
            recv_sem=hand_recv.at[p],
            device_id=(gx, to),
            device_id_type=MESH,
        )

    def pack(p):
        for c in range(2):
            keep = (amount[p] > c).astype(f32).astype(bf16)
            packed[2 * p + c] = final[jnp.minimum(begin[p] + c, BINS - 1)] * keep

    def step_two(i, carry):
        for c in range(2):
            final[2 * i + c] = mix(second, order[2 * i + c])
        pack(i)
        give(i).start()
        return carry

    lax.fori_loop(0, BINS // 2, step_two, 0)

    def rest(p, carry):
        pack(p)
        give(p).start()
        return carry

    lax.fori_loop(BINS // 2, n_gy - 1, rest, 0)
    pack(n_gy - 1)
    stay = pltpu.make_async_copy(
        packed.at[pl.ds(2 * n_gy - 2, 2)], out.at[pl.ds(2 * gy, 2)], own_sem.at[1]
    )
    stay.start()

    for copy in pos_copies + load_copies:
        copy.wait_send()

    def sent(i, carry):
        for copy in halo(i):
            copy.wait_send()
        return carry

    lax.fori_loop(0, BX, sent, 0)

    def taken(p, carry):
        give(p).wait()
        return carry

    lax.fori_loop(0, n_gy - 1, taken, 0)
    stay.wait()


def body(n_gx, n_gy, load, pos, kelvin, factor, onset, codes, zone):
    species, walkers = load.shape[1:]
    smem = pl.BlockSpec(memory_space=pltpu.SMEM)
    vmem = pl.BlockSpec(memory_space=pltpu.VMEM)
    anywhere = pl.BlockSpec(memory_space=pl.ANY)
    dma = pltpu.SemaphoreType.DMA
    return pl.pallas_call(
        functools.partial(kernel, n_gx, n_gy),
        out_shape=jax.ShapeDtypeStruct((2 * n_gy, species, walkers), bf16),
        in_specs=[smem, smem, vmem, vmem, vmem, vmem, anywhere],
        out_specs=anywhere,
        scratch_shapes=[
            pltpu.VMEM((BX, BY, 3, walkers), f32),
            pltpu.VMEM((EX, EY, 3, walkers), f32),
            pltpu.VMEM((EX * EY // 2, walkers, 128), bf16),
            pltpu.VMEM((BINS * NBR, walkers, walkers), bf16),
            pltpu.VMEM((BINS, 8, walkers), f32),
            pltpu.VMEM((EX, EY, species, walkers), bf16),
            pltpu.VMEM((EX, EY, species, walkers), bf16),
            pltpu.VMEM((BINS, species, walkers), bf16),
            pltpu.VMEM((2 * n_gy, species, walkers), bf16),
            pltpu.SMEM((n_gy,), jnp.int32),
            pltpu.SMEM((BINS,), jnp.int32),
            pltpu.SMEM((n_gy,), jnp.int32),
            pltpu.SMEM((n_gy,), jnp.int32),
            dma((2,)),
            dma((8,)),
            dma((8,)),
            dma((8,)),
            dma((8,)),
            dma((5, BX)),
            dma((5, BX)),
            dma((n_gy,)),
            dma((n_gy,)),
        ],
        compiler_params=pltpu.CompilerParams(
            collective_id=0, has_side_effects=True, vmem_limit_bytes=67043328
        ),
    )(
        codes,
        zone.reshape(1, -1),
        pos.transpose(1, 0, 2),
        kelvin,
        factor.reshape(1, -1),
        onset.reshape(1, -1),
        load.reshape(BX, BY, species, walkers),
    )


def solution(mesh):
    both = ("gx", "gy")
    in_specs = (
        P(both, None, None),
        P(both, None, None),
        P(both, None),
        P(),
        P(),
        P(both, None),
        P(both, None),
    )
    return jax.shard_map(
        functools.partial(body, mesh.shape["gx"], mesh.shape["gy"]),
        mesh=mesh,
        in_specs=in_specs,
        out_specs=P(both, None, None),
        check_vma=False,
    )
```

```python
import functools

import jax
import jax.numpy as jnp
from jax import lax
from jax.experimental import pallas as pl
from jax.experimental.pallas import tpu as pltpu
from jax.sharding import PartitionSpec as P

BX = 4
BY = 4
NBR = 16
BINS = BX * BY
EX = BX + 4
EY = BY + 4
SHARPNESS = 4.0 * 1.4426950408889634
FAR = -100000.0
MESH = pl.DeviceIdType.MESH
f32 = jnp.float32
bf16 = jnp.bfloat16

STEPS8 = [(0, 1), (0, -1), (1, 0), (-1, 0), (1, 1), (1, -1), (-1, 1), (-1, -1)]


SIDE = 4


def hops(step):
    return min(step, SIDE - step)


HANDS = sorted(
    ((ox, oz) for ox in range(SIDE) for oz in range(SIDE)),
    key=lambda step: (-hops(step[0]) - hops(step[1]), step),
)


def split3(x):
    x1 = x.astype(bf16).astype(f32)
    rest = x - x1
    x2 = rest.astype(bf16).astype(f32)
    x3 = (rest - x2).astype(bf16).astype(f32)
    return x1, x2, x3


def span(step, size):
    if step == 1:
        return size - 2, 2, 0
    if step == -1:
        return 0, 2, size + 2
    return 0, size, 2


def kernel(
    n_gx,
    n_gy,
    codes_in,
    zone_in,
    planes_in,
    kelvin_in,
    factor_in,
    onset_in,
    load,
    out,
    codes,
    zone,
    planes,
    kelvin,
    factor,
    onset,
    pos,
    posx,
    points,
    tiles,
    totals,
    first,
    second,
    final,
    packed,
    place_of,
    order,
    begin,
    amount,
    own_sem,
    pos_send,
    pos_recv,
    load_send,
    load_recv,
    halo_send,
    halo_recv,
    hand_send,
    hand_recv,
):
    gx = lax.axis_index("gx")
    gy = lax.axis_index("gy")

    def at(dx, dy):
        return (lax.rem(gx + dx + n_gx, n_gx), lax.rem(gy + dy + n_gy, n_gy))

    barrier = pltpu.get_barrier_semaphore()
    partners = [(dx, dy) for dx, dy in STEPS8] + [(0, r) for r in range(2, n_gy - 1)]
    for dx, dy in partners:
        pl.semaphore_signal(barrier, inc=1, device_id=at(dx, dy), device_id_type=MESH)

    fetches = [
        pltpu.make_async_copy(source, here, own_sem.at[number + 2])
        for number, (source, here) in enumerate(
            [
                (planes_in, planes),
                (codes_in, codes),
                (zone_in, zone),
                (kelvin_in, kelvin),
                (factor_in, factor),
                (onset_in, onset),
            ]
        )
    ]
    for fetch in fetches:
        fetch.start()
    own_load = pltpu.make_async_copy(load, first.at[pl.ds(2, BX), pl.ds(2, BY)], own_sem.at[0])
    own_load.start()
    fetches[0].wait()
    for b in range(BINS):
        mine = jnp.concatenate([planes[c, pl.ds(b, 1)] for c in range(3)], axis=0)
        pos[b // BY, b % BY] = mine
        posx[b // BY + 2, b % BY + 2] = mine

    pl.semaphore_wait(barrier, len(partners))

    def swap(source, framed, send, recv):
        copies = []
        for number, (dx, dy) in enumerate(STEPS8):
            row, rows, to_row = span(dx, BX)
            col, cols, to_col = span(dy, BY)
            copies.append(
                pltpu.make_async_remote_copy(
                    src_ref=source.at[pl.ds(row, rows), pl.ds(col, cols)],
                    dst_ref=framed.at[pl.ds(to_row, rows), pl.ds(to_col, cols)],
                    send_sem=send.at[number],
                    recv_sem=recv.at[number],
                    device_id=at(dx, dy),
                    device_id_type=MESH,
                )
            )
        for copy in copies:
            copy.start()
        return copies

    me_x = gy // SIDE
    me_z = lax.rem(gy, SIDE)

    def target(p):
        over_x = jnp.int32(0)
        over_z = jnp.int32(0)
        for number, (ox, oz) in enumerate(HANDS):
            over_x = jnp.where(p == number, ox, over_x)
            over_z = jnp.where(p == number, oz, over_z)
        return lax.rem(me_x + over_x, SIDE) * SIDE + lax.rem(me_z + over_z, SIDE)

    pos_copies = swap(pos, posx, pos_send, pos_recv)
    load_copies = swap(load, first, load_send, load_recv)

    for fetch in fetches[1:]:
        fetch.wait()

    eye = lax.broadcasted_iota(jnp.int32, (32, 32), 0) == lax.broadcasted_iota(
        jnp.int32, (32, 32), 1
    )

    def column(ref):
        return jnp.sum(jnp.where(eye, ref[...], 0.0), axis=1, keepdims=True)

    factors = column(factor)
    onsets = column(onset)

    for number, (ox, oz) in enumerate(HANDS):
        place_of[ox * SIDE + oz] = jnp.int32(number)
    places = []
    for b in range(BINS):
        to = zone[0, b]
        over_x = ((to >> 2) - me_x) & 3
        over_z = ((to & 3) - me_z) & 3
        places.append(place_of[over_x * SIDE + over_z])
    ranks = [jnp.int32(0) for _ in range(BINS)]
    for b in range(BINS):
        for c in range(b):
            ahead = (places[c] <= places[b]).astype(jnp.int32)
            ranks[b] = ranks[b] + ahead
            ranks[c] = ranks[c] + (1 - ahead)
    for i in range(BINS):
        bin_at = jnp.int32(0)
        for b in range(BINS):
            bin_at = jnp.where(ranks[b] == i, b, bin_at)
        order[i] = bin_at
    before = jnp.int32(0)
    for p in range(n_gy):
        here = jnp.int32(0)
        for b in range(BINS):
            here = here + (places[b] == p).astype(jnp.int32)
        begin[p] = before
        amount[p] = here
        before = before + here

    row8 = lax.broadcasted_iota(jnp.int32, (8, 256), 0)
    none = jnp.zeros((5, 256), f32)

    def point_rows(x, y):
        where = jnp.concatenate([posx[x, y], none], axis=0)
        norm = -SHARPNESS * jnp.sum(where * where, axis=0, keepdims=True)
        rows = jnp.where(row8 == 3, 1.0, jnp.where(row8 == 4, norm, where))
        p1, p2, p3 = split3(rows)
        return jnp.concatenate([p1, p2, p1, p2, p3, p1, jnp.zeros((16, 256), f32)], axis=0)

    def prepare(x, pair):
        rows = jnp.concatenate(
            [point_rows(x, 2 * pair), point_rows(x, 2 * pair + 1)], axis=0
        )
        points[x * (EY // 2) + pair] = rows.T.astype(bf16)

    def prepare_own(i, carry):
        for x in range(2):
            for pair in range(1, EY // 2 - 1):
                prepare(2 * i + x + 2, pair)
        return carry

    def prepare_sides(i, carry):
        for x in range(2):
            for pair in (0, EY // 2 - 1):
                prepare(2 * i + x + 2, pair)
        return carry

    def prepare_ends(i, carry):
        for x in range(2):
            for pair in range(EY // 2):
                prepare(i * (BX + 2) + x, pair)
        return carry

    def neighbour(b, k):
        code = codes[b, k]
        along = ((code * 13) >> 6) - 2
        across = code - (along + 2) * 5 - 2
        inside_x = gx * BX + b // BY + along
        inside_y = gy * BY + b % BY + across
        inside = (
            (inside_x >= 0)
            & (inside_x < n_gx * BX)
            & (inside_y >= 0)
            & (inside_y < n_gy * BY)
        )
        return along, across, inside

    def weigh_tile(b, k, own, along, across, inside):
        place = (b // BY + 2 + along) * EY + b % BY + 2 + across
        odd = (place & 1).astype(f32)
        shift = jnp.where(
            row8 == 0, along.astype(f32), jnp.where(row8 == 1, across.astype(f32), 0.0)
        )
        there = own - shift
        norm = -SHARPNESS * jnp.sum(there * there, axis=0, keepdims=True)
        norm = norm + jnp.where(inside, 0.0, FAR)
        rows = jnp.where(row8 == 3, norm, jnp.where(row8 == 4, 1.0, there * (2.0 * SHARPNESS)))
        p1, p2, p3 = split3(rows)
        rows = jnp.concatenate(
            [p1, p1, p2, p2, p1, p3, jnp.zeros((16, 256), f32)], axis=0
        ).astype(bf16)
        rows = jnp.concatenate(
            [rows * (1.0 - odd).astype(bf16), rows * odd.astype(bf16)], axis=0
        )
        tile = jnp.exp2(jnp.dot(points[place >> 1], rows, preferred_element_type=f32))
        tiles[b * NBR + k] = tile.astype(bf16)
        return jnp.sum(tile.reshape(32, 8, 256), axis=0)

    def weigh_self(i, carry):
        for c in range(8):
            b = i * 8 + c
            own = jnp.concatenate([pos[b // BY, b % BY], none], axis=0)
            still = jnp.int32(0)
            totals[b] = weigh_tile(b, 0, own, still, still, True)
        return carry

    def weigh(i, carry):
        for c in range(2):
            b = i * 2 + c
            own = jnp.concatenate([pos[b // BY, b % BY], none], axis=0)
            total = totals[b]
            for k in range(1, NBR):
                total = total + weigh_tile(b, k, own, *neighbour(b, k))
            totals[b] = total
        return carry

    lax.fori_loop(0, 2, prepare_own, 0)
    lax.fori_loop(0, 2, weigh_self, 0)
    for copy in pos_copies:
        copy.wait_recv()
    lax.fori_loop(0, 2, prepare_sides, 0)
    lax.fori_loop(0, 2, prepare_ends, 0)

    lax.fori_loop(0, BINS // 2, weigh, 0)

    def mix(framed, b):
        sources = []
        for k in range(NBR):
            along, across, _ = neighbour(b, k)
            sources.append(framed[b // BY + 2 + along, b % BY + 2 + across])
        sources = jnp.concatenate(sources, axis=1)
        weights = tiles[pl.ds(b * NBR, NBR)].reshape(NBR * 256, 256)
        mixture = jnp.dot(sources, weights, preferred_element_type=f32)
        mixture = mixture / jnp.sum(totals[b], axis=0, keepdims=True)
        speed = factors * jnp.exp(-onsets / kelvin[pl.ds(b, 1)])
        u = mixture[:32]
        v = mixture[32:]
        reacted = speed * u * v / (1.0 + speed * (u + v))
        return jnp.concatenate([u - reacted, v - reacted], axis=0).astype(bf16)

    own_load.wait()
    for copy in load_copies:
        copy.wait_recv()

    parity = lax.rem(gx, 2)

    def row_at(i):
        return i + parity * (BX - 1 - 2 * i)

    def remote(kind, i, row, col, cols, to_row, to_col, sx, sy):
        return pltpu.make_async_remote_copy(
            src_ref=second.at[row, pl.ds(col, cols)],
            dst_ref=second.at[to_row, pl.ds(to_col, cols)],
            send_sem=halo_send.at[kind, i],
            recv_sem=halo_recv.at[kind, i],
            device_id=at(sx, sy),
            device_id_type=MESH,
        )

    def sides(i):
        row = row_at(i) + 2
        return [
            remote(0, i, row, 2, 2, row, BY + 2, 0, -1),
            remote(1, i, row, BY, 2, row, 0, 0, 1),
        ]

    def along(i, kinds):
        row = row_at(i) + 2
        dx = (row_at(i) // 2) * 2 - 1
        spans = {2: (2, BY), 3: (0, 2), 4: (BY + 2, 2)}
        return [
            remote(kind, i, row, *spans[kind], row - BX * dx, spans[kind][0], dx, 0)
            for kind in kinds
        ]

    def pass_on(i):
        for copy in sides(i):
            copy.wait_recv()
        for copy in along(i, (3, 4)):
            copy.start()

    def mix_row(i):
        for j in range(BY):
            second[row_at(i) + 2, j + 2] = mix(first, row_at(i) * BY + j)
        for copy in sides(i) + along(i, (2,)):
            copy.start()

    def early_row(i, carry):
        mix_row(i)
        return carry

    def late_row(i, carry):
        mix_row(i)
        pass_on(i - BX // 2)
        return carry

    lax.fori_loop(0, BX // 2, early_row, 0)
    lax.fori_loop(BX // 2, BX, late_row, 0)
    for i in range(BX // 2, BX):
        pass_on(i)
    for i in range(BX):
        for copy in along(i, (2, 3, 4)):
            copy.wait_recv()

    def give(p):
        to = target(p)
        return pltpu.make_async_remote_copy(
            src_ref=packed.at[pl.ds(2 * p, 2)],
            dst_ref=out.at[pl.ds(2 * gy, 2)],
            send_sem=hand_send.at[p],
            recv_sem=hand_recv.at[p],
            device_id=(gx, to),
            device_id_type=MESH,
        )

    def pack(p):
        for c in range(2):
            keep = (amount[p] > c).astype(f32).astype(bf16)
            packed[2 * p + c] = final[jnp.minimum(begin[p] + c, BINS - 1)] * keep

    def step_two(i, carry):
        for c in range(2):
            final[2 * i + c] = mix(second, order[2 * i + c])
        pack(i)
        give(i).start()
        return carry

    lax.fori_loop(0, BINS // 2, step_two, 0)

    def rest(p, carry):
        pack(p)
        give(p).start()
        return carry

    lax.fori_loop(BINS // 2, n_gy - 1, rest, 0)
    pack(n_gy - 1)
    stay = pltpu.make_async_copy(
        packed.at[pl.ds(2 * n_gy - 2, 2)], out.at[pl.ds(2 * gy, 2)], own_sem.at[1]
    )
    stay.start()

    for copy in pos_copies + load_copies:
        copy.wait_send()
    for i in range(BX):
        for copy in sides(i) + along(i, (2, 3, 4)):
            copy.wait_send()

    def taken(p, carry):
        give(p).wait()
        return carry

    lax.fori_loop(0, n_gy - 1, taken, 0)
    stay.wait()


def body(n_gx, n_gy, load, pos, kelvin, factor, onset, codes, zone):
    species, walkers = load.shape[1:]
    anywhere = pl.BlockSpec(memory_space=pl.ANY)
    dma = pltpu.SemaphoreType.DMA
    return pl.pallas_call(
        functools.partial(kernel, n_gx, n_gy),
        out_shape=jax.ShapeDtypeStruct((2 * n_gy, species, walkers), bf16),
        in_specs=[anywhere] * 7,
        out_specs=anywhere,
        scratch_shapes=[
            pltpu.SMEM((BINS, NBR), jnp.int32),
            pltpu.SMEM((1, BINS), jnp.int32),
            pltpu.VMEM((3, BINS, walkers), f32),
            pltpu.VMEM((BINS, walkers), f32),
            pltpu.VMEM((1, species // 2), f32),
            pltpu.VMEM((1, species // 2), f32),
            pltpu.VMEM((BX, BY, 3, walkers), f32),
            pltpu.VMEM((EX, EY, 3, walkers), f32),
            pltpu.VMEM((EX * EY // 2, walkers, 128), bf16),
            pltpu.VMEM((BINS * NBR, walkers, walkers), bf16),
            pltpu.VMEM((BINS, 8, walkers), f32),
            pltpu.VMEM((EX, EY, species, walkers), bf16),
            pltpu.VMEM((EX, EY, species, walkers), bf16),
            pltpu.VMEM((BINS, species, walkers), bf16),
            pltpu.VMEM((2 * n_gy, species, walkers), bf16),
            pltpu.SMEM((n_gy,), jnp.int32),
            pltpu.SMEM((BINS,), jnp.int32),
            pltpu.SMEM((n_gy,), jnp.int32),
            pltpu.SMEM((n_gy,), jnp.int32),
            dma((8,)),
            dma((8,)),
            dma((8,)),
            dma((8,)),
            dma((8,)),
            dma((5, BX)),
            dma((5, BX)),
            dma((n_gy,)),
            dma((n_gy,)),
        ],
        compiler_params=pltpu.CompilerParams(
            collective_id=0, has_side_effects=True, vmem_limit_bytes=67043328
        ),
    )(
        codes,
        zone.reshape(1, -1),
        pos.transpose(1, 0, 2),
        kelvin,
        factor.reshape(1, -1),
        onset.reshape(1, -1),
        load.reshape(BX, BY, species, walkers),
    )


def solution(mesh):
    both = ("gx", "gy")
    in_specs = (
        P(both, None, None),
        P(both, None, None),
        P(both, None),
        P(),
        P(),
        P(both, None),
        P(both, None),
    )
    return jax.shard_map(
        functools.partial(body, mesh.shape["gx"], mesh.shape["gy"]),
        mesh=mesh,
        in_specs=in_specs,
        out_specs=P(both, None, None),
        check_vma=False,
    )
```

```python
import functools

import jax
import jax.numpy as jnp
from jax import lax
from jax.experimental import pallas as pl
from jax.experimental.pallas import tpu as pltpu
from jax.sharding import PartitionSpec as P

BX = 4
BY = 4
NBR = 16
BINS = BX * BY
EX = BX + 4
EY = BY + 4
SHARPNESS = 4.0 * 1.4426950408889634
FAR = -100000.0
MESH = pl.DeviceIdType.MESH
f32 = jnp.float32
bf16 = jnp.bfloat16

STEPS8 = [(0, 1), (0, -1), (1, 0), (-1, 0), (1, 1), (1, -1), (-1, 1), (-1, -1)]


SIDE = 4


def hops(step):
    return min(step, SIDE - step)


HANDS = sorted(
    ((ox, oz) for ox in range(SIDE) for oz in range(SIDE)),
    key=lambda step: (-hops(step[0]) - hops(step[1]), step),
)


def split3(x):
    x1 = x.astype(bf16).astype(f32)
    rest = x - x1
    x2 = rest.astype(bf16).astype(f32)
    x3 = (rest - x2).astype(bf16).astype(f32)
    return x1, x2, x3


def span(step, size):
    if step == 1:
        return size - 2, 2, 0
    if step == -1:
        return 0, 2, size + 2
    return 0, size, 2


def kernel(
    n_gx,
    n_gy,
    codes_in,
    zone_in,
    planes_in,
    kelvin_in,
    factor_in,
    onset_in,
    load,
    out,
    codes,
    zone,
    planes,
    kelvin,
    factor,
    onset,
    pos,
    posx,
    points,
    tiles,
    totals,
    first,
    second,
    final,
    packed,
    place_of,
    order,
    begin,
    amount,
    own_sem,
    pos_send,
    pos_recv,
    load_send,
    load_recv,
    halo_send,
    halo_recv,
    hand_send,
    hand_recv,
):
    gx = lax.axis_index("gx")
    gy = lax.axis_index("gy")

    def at(dx, dy):
        return (lax.rem(gx + dx + n_gx, n_gx), lax.rem(gy + dy + n_gy, n_gy))

    barrier = pltpu.get_barrier_semaphore()
    partners = [(dx, dy) for dx, dy in STEPS8] + [(0, r) for r in range(2, n_gy - 1)]
    for dx, dy in partners:
        pl.semaphore_signal(barrier, inc=1, device_id=at(dx, dy), device_id_type=MESH)

    fetches = [
        pltpu.make_async_copy(source, here, own_sem.at[number + 2])
        for number, (source, here) in enumerate(
            [
                (planes_in, planes),
                (codes_in, codes),
                (zone_in, zone),
                (kelvin_in, kelvin),
                (factor_in, factor),
                (onset_in, onset),
            ]
        )
    ]
    for fetch in fetches:
        fetch.start()
    own_load = pltpu.make_async_copy(load, first.at[pl.ds(2, BX), pl.ds(2, BY)], own_sem.at[0])
    own_load.start()
    fetches[0].wait()
    for b in range(BINS):
        mine = jnp.concatenate([planes[c, pl.ds(b, 1)] for c in range(3)], axis=0)
        pos[b // BY, b % BY] = mine
        posx[b // BY + 2, b % BY + 2] = mine

    pl.semaphore_wait(barrier, len(partners))

    def swap(source, framed, send, recv):
        copies = []
        for number, (dx, dy) in enumerate(STEPS8):
            row, rows, to_row = span(dx, BX)
            col, cols, to_col = span(dy, BY)
            copies.append(
                pltpu.make_async_remote_copy(
                    src_ref=source.at[pl.ds(row, rows), pl.ds(col, cols)],
                    dst_ref=framed.at[pl.ds(to_row, rows), pl.ds(to_col, cols)],
                    send_sem=send.at[number],
                    recv_sem=recv.at[number],
                    device_id=at(dx, dy),
                    device_id_type=MESH,
                )
            )
        for copy in copies:
            copy.start()
        return copies

    me_x = gy // SIDE
    me_z = lax.rem(gy, SIDE)

    def target(p):
        over_x = jnp.int32(0)
        over_z = jnp.int32(0)
        for number, (ox, oz) in enumerate(HANDS):
            over_x = jnp.where(p == number, ox, over_x)
            over_z = jnp.where(p == number, oz, over_z)
        return lax.rem(me_x + over_x, SIDE) * SIDE + lax.rem(me_z + over_z, SIDE)

    pos_copies = swap(pos, posx, pos_send, pos_recv)
    load_copies = swap(load, first, load_send, load_recv)

    for fetch in fetches[1:]:
        fetch.wait()

    eye = lax.broadcasted_iota(jnp.int32, (32, 32), 0) == lax.broadcasted_iota(
        jnp.int32, (32, 32), 1
    )

    def column(ref):
        return jnp.sum(jnp.where(eye, ref[...], 0.0), axis=1, keepdims=True)

    factors = column(factor)
    onsets = column(onset)

    for number, (ox, oz) in enumerate(HANDS):
        place_of[ox * SIDE + oz] = jnp.int32(number)
    places = []
    for b in range(BINS):
        to = zone[0, b]
        over_x = ((to >> 2) - me_x) & 3
        over_z = ((to & 3) - me_z) & 3
        places.append(place_of[over_x * SIDE + over_z])
    ranks = [jnp.int32(0) for _ in range(BINS)]
    for b in range(BINS):
        for c in range(b):
            ahead = (places[c] <= places[b]).astype(jnp.int32)
            ranks[b] = ranks[b] + ahead
            ranks[c] = ranks[c] + (1 - ahead)
    for i in range(BINS):
        bin_at = jnp.int32(0)
        for b in range(BINS):
            bin_at = jnp.where(ranks[b] == i, b, bin_at)
        order[i] = bin_at
    before = jnp.int32(0)
    for p in range(n_gy):
        here = jnp.int32(0)
        for b in range(BINS):
            here = here + (places[b] == p).astype(jnp.int32)
        begin[p] = before
        amount[p] = here
        before = before + here

    row8 = lax.broadcasted_iota(jnp.int32, (8, 256), 0)
    none = jnp.zeros((5, 256), f32)

    def point_rows(x, y):
        where = jnp.concatenate([posx[x, y], none], axis=0)
        norm = -SHARPNESS * jnp.sum(where * where, axis=0, keepdims=True)
        rows = jnp.where(row8 == 3, 1.0, jnp.where(row8 == 4, norm, where))
        p1, p2, p3 = split3(rows)
        return jnp.concatenate([p1, p2, p1, p2, p3, p1, jnp.zeros((16, 256), f32)], axis=0)

    def prepare(x, pair):
        rows = jnp.concatenate(
            [point_rows(x, 2 * pair), point_rows(x, 2 * pair + 1)], axis=0
        )
        points[x * (EY // 2) + pair] = rows.T.astype(bf16)

    def prepare_own(i, carry):
        for x in range(2):
            for pair in range(1, EY // 2 - 1):
                prepare(2 * i + x + 2, pair)
        return carry

    def prepare_sides(i, carry):
        for x in range(2):
            for pair in (0, EY // 2 - 1):
                prepare(2 * i + x + 2, pair)
        return carry

    def prepare_ends(i, carry):
        for pair in range(EY // 2):
            prepare(i + BX * (i // 2), pair)
        return carry

    def neighbour(b, k):
        code = codes[b, k]
        along = ((code * 13) >> 6) - 2
        across = code - (along + 2) * 5 - 2
        inside_x = gx * BX + b // BY + along
        inside_y = gy * BY + b % BY + across
        inside = (
            (inside_x >= 0)
            & (inside_x < n_gx * BX)
            & (inside_y >= 0)
            & (inside_y < n_gy * BY)
        )
        return along, across, inside

    def weigh_tile(b, k, own, along, across, inside):
        place = (b // BY + 2 + along) * EY + b % BY + 2 + across
        odd = (place & 1).astype(f32)
        shift = jnp.where(
            row8 == 0, along.astype(f32), jnp.where(row8 == 1, across.astype(f32), 0.0)
        )
        there = own - shift
        norm = -SHARPNESS * jnp.sum(there * there, axis=0, keepdims=True)
        norm = norm + jnp.where(inside, 0.0, FAR)
        rows = jnp.where(row8 == 3, norm, jnp.where(row8 == 4, 1.0, there * (2.0 * SHARPNESS)))
        p1, p2, p3 = split3(rows)
        rows = jnp.concatenate(
            [p1, p1, p2, p2, p1, p3, jnp.zeros((16, 256), f32)], axis=0
        ).astype(bf16)
        rows = jnp.concatenate(
            [rows * (1.0 - odd).astype(bf16), rows * odd.astype(bf16)], axis=0
        )
        tile = jnp.exp2(jnp.dot(points[place >> 1], rows, preferred_element_type=f32))
        tiles[b * NBR + k] = tile.astype(bf16)
        return jnp.sum(tile.reshape(32, 8, 256), axis=0)

    def weigh_self(i, carry):
        for c in range(8):
            b = i * 8 + c
            own = jnp.concatenate([pos[b // BY, b % BY], none], axis=0)
            still = jnp.int32(0)
            totals[b] = weigh_tile(b, 0, own, still, still, True)
        return carry

    def weigh(i, carry):
        for c in range(2):
            b = i * 2 + c
            own = jnp.concatenate([pos[b // BY, b % BY], none], axis=0)
            total = totals[b]
            for k in range(1, NBR):
                total = total + weigh_tile(b, k, own, *neighbour(b, k))
            totals[b] = total
        return carry

    lax.fori_loop(0, 2, prepare_own, 0)
    lax.fori_loop(0, 2, weigh_self, 0)
    for copy in pos_copies:
        copy.wait_recv()
    lax.fori_loop(0, 2, prepare_sides, 0)
    lax.fori_loop(0, 4, prepare_ends, 0)

    lax.fori_loop(0, BINS // 2, weigh, 0)

    def mix(framed, b):
        sources = []
        for k in range(NBR):
            along, across, _ = neighbour(b, k)
            sources.append(framed[b // BY + 2 + along, b % BY + 2 + across])
        sources = jnp.concatenate(sources, axis=1)
        weights = tiles[pl.ds(b * NBR, NBR)].reshape(NBR * 256, 256)
        mixture = jnp.dot(sources, weights, preferred_element_type=f32)
        mixture = mixture / jnp.sum(totals[b], axis=0, keepdims=True)
        speed = factors * jnp.exp(-onsets / kelvin[pl.ds(b, 1)])
        u = mixture[:32]
        v = mixture[32:]
        reacted = speed * u * v / (1.0 + speed * (u + v))
        return jnp.concatenate([u - reacted, v - reacted], axis=0).astype(bf16)

    own_load.wait()
    for copy in load_copies:
        copy.wait_recv()

    parity = lax.rem(gx, 2)

    def row_at(i):
        return i + parity * (BX - 1 - 2 * i)

    def remote(kind, i, row, col, cols, to_row, to_col, sx, sy):
        return pltpu.make_async_remote_copy(
            src_ref=second.at[row, pl.ds(col, cols)],
            dst_ref=second.at[to_row, pl.ds(to_col, cols)],
            send_sem=halo_send.at[kind, i],
            recv_sem=halo_recv.at[kind, i],
            device_id=at(sx, sy),
            device_id_type=MESH,
        )

    def sides(i):
        row = row_at(i) + 2
        return [
            remote(0, i, row, 2, 2, row, BY + 2, 0, -1),
            remote(1, i, row, BY, 2, row, 0, 0, 1),
        ]

    def along(i, kinds):
        row = row_at(i) + 2
        dx = (row_at(i) // 2) * 2 - 1
        spans = {2: (2, BY), 3: (0, 2), 4: (BY + 2, 2)}
        return [
            remote(kind, i, row, *spans[kind], row - BX * dx, spans[kind][0], dx, 0)
            for kind in kinds
        ]

    def pass_on(i):
        for copy in sides(i):
            copy.wait_recv()
        for copy in along(i, (3, 4)):
            copy.start()

    def mix_row(i, carry):
        for j in range(BY):
            second[row_at(i) + 2, j + 2] = mix(first, row_at(i) * BY + j)
        for copy in sides(i) + along(i, (2,)):
            copy.start()

        @pl.when(i >= BX // 2)
        def _():
            pass_on(i - BX // 2)

        return carry

    lax.fori_loop(0, BX, mix_row, 0)
    for i in range(BX // 2, BX):
        pass_on(i)
    for i in range(BX):
        for copy in along(i, (2, 3, 4)):
            copy.wait_recv()

    def give(p):
        to = target(p)
        return pltpu.make_async_remote_copy(
            src_ref=packed.at[pl.ds(2 * p, 2)],
            dst_ref=out.at[pl.ds(2 * gy, 2)],
            send_sem=hand_send.at[p],
            recv_sem=hand_recv.at[p],
            device_id=(gx, to),
            device_id_type=MESH,
        )

    def pack(p):
        for c in range(2):
            keep = (amount[p] > c).astype(f32).astype(bf16)
            packed[2 * p + c] = final[jnp.minimum(begin[p] + c, BINS - 1)] * keep

    def step_two(i, carry):
        for c in range(2):
            final[2 * i + c] = mix(second, order[2 * i + c])
        pack(i)
        give(i).start()
        return carry

    lax.fori_loop(0, BINS // 2, step_two, 0)

    def rest(p, carry):
        pack(p)
        give(p).start()
        return carry

    lax.fori_loop(BINS // 2, n_gy - 1, rest, 0)
    pack(n_gy - 1)
    stay = pltpu.make_async_copy(
        packed.at[pl.ds(2 * n_gy - 2, 2)], out.at[pl.ds(2 * gy, 2)], own_sem.at[1]
    )
    stay.start()

    for copy in pos_copies + load_copies:
        copy.wait_send()
    for i in range(BX):
        for copy in sides(i) + along(i, (2, 3, 4)):
            copy.wait_send()

    def taken(p, carry):
        give(p).wait()
        return carry

    lax.fori_loop(0, n_gy - 1, taken, 0)
    stay.wait()


def body(n_gx, n_gy, load, pos, kelvin, factor, onset, codes, zone):
    species, walkers = load.shape[1:]
    anywhere = pl.BlockSpec(memory_space=pl.ANY)
    dma = pltpu.SemaphoreType.DMA
    return pl.pallas_call(
        functools.partial(kernel, n_gx, n_gy),
        out_shape=pltpu.VMEM((2 * n_gy, species, walkers), bf16),
        in_specs=[anywhere] * 7,
        out_specs=pl.BlockSpec(memory_space=pltpu.VMEM),
        scratch_shapes=[
            pltpu.SMEM((BINS, NBR), jnp.int32),
            pltpu.SMEM((1, BINS), jnp.int32),
            pltpu.VMEM((3, BINS, walkers), f32),
            pltpu.VMEM((BINS, walkers), f32),
            pltpu.VMEM((1, species // 2), f32),
            pltpu.VMEM((1, species // 2), f32),
            pltpu.VMEM((BX, BY, 3, walkers), f32),
            pltpu.VMEM((EX, EY, 3, walkers), f32),
            pltpu.VMEM((EX * EY // 2, walkers, 128), bf16),
            pltpu.VMEM((BINS * NBR, walkers, walkers), bf16),
            pltpu.VMEM((BINS, 8, walkers), f32),
            pltpu.VMEM((EX, EY, species, walkers), bf16),
            pltpu.VMEM((EX, EY, species, walkers), bf16),
            pltpu.VMEM((BINS, species, walkers), bf16),
            pltpu.VMEM((2 * n_gy, species, walkers), bf16),
            pltpu.SMEM((n_gy,), jnp.int32),
            pltpu.SMEM((BINS,), jnp.int32),
            pltpu.SMEM((n_gy,), jnp.int32),
            pltpu.SMEM((n_gy,), jnp.int32),
            dma((8,)),
            dma((8,)),
            dma((8,)),
            dma((8,)),
            dma((8,)),
            dma((5, BX)),
            dma((5, BX)),
            dma((n_gy,)),
            dma((n_gy,)),
        ],
        compiler_params=pltpu.CompilerParams(
            collective_id=0, has_side_effects=True, vmem_limit_bytes=56 * 1024 * 1024
        ),
    )(
        codes,
        zone.reshape(1, -1),
        pos.transpose(1, 0, 2),
        kelvin,
        factor.reshape(1, -1),
        onset.reshape(1, -1),
        load.reshape(BX, BY, species, walkers),
    )


def solution(mesh):
    both = ("gx", "gy")
    in_specs = (
        P(both, None, None),
        P(both, None, None),
        P(both, None),
        P(),
        P(),
        P(both, None),
        P(both, None),
    )
    return jax.shard_map(
        functools.partial(body, mesh.shape["gx"], mesh.shape["gy"]),
        mesh=mesh,
        in_specs=in_specs,
        out_specs=P(both, None, None),
        check_vma=False,
    )
```

```python
import functools

import jax
import jax.numpy as jnp
from jax import lax
from jax.experimental import pallas as pl
from jax.experimental.pallas import tpu as pltpu
from jax.sharding import PartitionSpec as P

BX = 4
BY = 4
NBR = 16
BINS = BX * BY
EX = BX + 4
EY = BY + 4
PASS_AFTER = (1, 3)
SHARPNESS = 4.0 * 1.4426950408889634
FAR = -100000.0
MESH = pl.DeviceIdType.MESH
f32 = jnp.float32
bf16 = jnp.bfloat16

STEPS8 = [(0, 1), (0, -1), (1, 0), (-1, 0), (1, 1), (1, -1), (-1, 1), (-1, -1)]


SIDE = 4


def hops(step):
    return min(step, SIDE - step)


HANDS = sorted(
    ((ox, oz) for ox in range(SIDE) for oz in range(SIDE)),
    key=lambda step: (-hops(step[0]) - hops(step[1]), step),
)


def split3(x):
    x1 = x.astype(bf16).astype(f32)
    rest = x - x1
    x2 = rest.astype(bf16).astype(f32)
    x3 = (rest - x2).astype(bf16).astype(f32)
    return x1, x2, x3


def span(step, size):
    if step == 1:
        return size - 2, 2, 0
    if step == -1:
        return 0, 2, size + 2
    return 0, size, 2


def kernel(
    n_gx,
    n_gy,
    codes_in,
    zone_in,
    planes_in,
    kelvin_in,
    factor_in,
    onset_in,
    load,
    out,
    codes,
    zone,
    planes,
    kelvin,
    factor,
    onset,
    pos,
    posx,
    points,
    tiles,
    totals,
    speeds,
    first,
    second,
    final,
    packed,
    place_of,
    order,
    begin,
    amount,
    own_sem,
    pos_send,
    pos_recv,
    load_send,
    load_recv,
    halo_send,
    halo_recv,
    hand_send,
    hand_recv,
):
    gx = lax.axis_index("gx")
    gy = lax.axis_index("gy")

    def at(dx, dy):
        return (lax.rem(gx + dx + n_gx, n_gx), lax.rem(gy + dy + n_gy, n_gy))

    barrier = pltpu.get_barrier_semaphore()
    partners = [(dx, dy) for dx, dy in STEPS8] + [(0, r) for r in range(2, n_gy - 1)]
    for dx, dy in partners:
        pl.semaphore_signal(barrier, inc=1, device_id=at(dx, dy), device_id_type=MESH)

    fetches = [
        pltpu.make_async_copy(source, here, own_sem.at[number + 2])
        for number, (source, here) in enumerate(
            [
                (planes_in, planes),
                (codes_in, codes),
                (zone_in, zone),
                (kelvin_in, kelvin),
                (factor_in, factor),
                (onset_in, onset),
            ]
        )
    ]
    for fetch in fetches:
        fetch.start()
    own_load = pltpu.make_async_copy(load, first.at[pl.ds(2, BX), pl.ds(2, BY)], own_sem.at[0])
    own_load.start()
    fetches[0].wait()
    for b in range(BINS):
        mine = jnp.concatenate([planes[c, pl.ds(b, 1)] for c in range(3)], axis=0)
        pos[b // BY, b % BY] = mine
        posx[b // BY + 2, b % BY + 2] = mine

    pl.semaphore_wait(barrier, len(partners))

    def swap(source, framed, send, recv):
        copies = []
        for number, (dx, dy) in enumerate(STEPS8):
            row, rows, to_row = span(dx, BX)
            col, cols, to_col = span(dy, BY)
            copies.append(
                pltpu.make_async_remote_copy(
                    src_ref=source.at[pl.ds(row, rows), pl.ds(col, cols)],
                    dst_ref=framed.at[pl.ds(to_row, rows), pl.ds(to_col, cols)],
                    send_sem=send.at[number],
                    recv_sem=recv.at[number],
                    device_id=at(dx, dy),
                    device_id_type=MESH,
                )
            )
        for copy in copies:
            copy.start()
        return copies

    me_x = gy // SIDE
    me_z = lax.rem(gy, SIDE)

    def target(p):
        over_x = jnp.int32(0)
        over_z = jnp.int32(0)
        for number, (ox, oz) in enumerate(HANDS):
            over_x = jnp.where(p == number, ox, over_x)
            over_z = jnp.where(p == number, oz, over_z)
        return lax.rem(me_x + over_x, SIDE) * SIDE + lax.rem(me_z + over_z, SIDE)

    pos_copies = swap(pos, posx, pos_send, pos_recv)

    parity = lax.rem(gx, 2)

    def load_copy(kind, half, source, row, col, cols, to_row, to_col, sx, sy):
        return pltpu.make_async_remote_copy(
            src_ref=source.at[pl.ds(row, 2), pl.ds(col, cols)],
            dst_ref=first.at[pl.ds(to_row, 2), pl.ds(to_col, cols)],
            send_sem=load_send.at[kind, half],
            recv_sem=load_recv.at[kind, half],
            device_id=at(sx, sy),
            device_id_type=MESH,
        )

    def load_row(half):
        return 2 * half + parity * (2 - 4 * half)

    def load_sides(half):
        row = load_row(half)
        return [
            load_copy(0, half, load, row, 0, 2, row + 2, BY + 2, 0, -1),
            load_copy(1, half, load, row, 2, 2, row + 2, 0, 0, 1),
        ]

    def load_along(half):
        row = load_row(half)
        dx = row - 1
        return [load_copy(2, half, load, row, 0, BY, row + 2 - BX * dx, 2, dx, 0)]

    def load_corners(half):
        row = load_row(half) + 2
        dx = row - 3
        return [
            load_copy(kind, half, first, row, col, 2, row - BX * dx, col, dx, 0)
            for kind, col in ((3, 0), (4, BY + 2))
        ]

    for half in range(2):
        for copy in load_sides(half) + load_along(half):
            copy.start()

    def pass_load(half):
        for copy in load_sides(half):
            copy.wait_recv()
        for copy in load_corners(half):
            copy.start()


    for fetch in fetches[1:]:
        fetch.wait()

    eye = lax.broadcasted_iota(jnp.int32, (32, 32), 0) == lax.broadcasted_iota(
        jnp.int32, (32, 32), 1
    )

    def column(ref):
        return jnp.sum(jnp.where(eye, ref[...], 0.0), axis=1, keepdims=True)

    factors = column(factor)
    onsets = column(onset)

    def quicken(i, carry):
        for c in range(4):
            b = i * 4 + c
            speeds[b] = factors * jnp.exp(-onsets / kelvin[pl.ds(b, 1)])
        return carry

    lax.fori_loop(0, BINS // 4, quicken, 0)

    for number, (ox, oz) in enumerate(HANDS):
        place_of[ox * SIDE + oz] = jnp.int32(number)
    places = []
    for b in range(BINS):
        to = zone[0, b]
        over_x = ((to >> 2) - me_x) & 3
        over_z = ((to & 3) - me_z) & 3
        places.append(place_of[over_x * SIDE + over_z])
    ranks = [jnp.int32(0) for _ in range(BINS)]
    for b in range(BINS):
        for c in range(b):
            ahead = (places[c] <= places[b]).astype(jnp.int32)
            ranks[b] = ranks[b] + ahead
            ranks[c] = ranks[c] + (1 - ahead)
    for i in range(BINS):
        bin_at = jnp.int32(0)
        for b in range(BINS):
            bin_at = jnp.where(ranks[b] == i, b, bin_at)
        order[i] = bin_at
    before = jnp.int32(0)
    for p in range(n_gy):
        here = jnp.int32(0)
        for b in range(BINS):
            here = here + (places[b] == p).astype(jnp.int32)
        begin[p] = before
        amount[p] = here
        before = before + here

    row8 = lax.broadcasted_iota(jnp.int32, (8, 256), 0)
    none = jnp.zeros((5, 256), f32)

    def point_rows(x, y):
        where = jnp.concatenate([posx[x, y], none], axis=0)
        norm = -SHARPNESS * jnp.sum(where * where, axis=0, keepdims=True)
        rows = jnp.where(row8 == 3, 1.0, jnp.where(row8 == 4, norm, where))
        p1, p2, p3 = split3(rows)
        return jnp.concatenate([p1, p2, p1, p2, p3, p1, jnp.zeros((16, 256), f32)], axis=0)

    def prepare(x, pair):
        rows = jnp.concatenate(
            [point_rows(x, 2 * pair), point_rows(x, 2 * pair + 1)], axis=0
        )
        points[x * (EY // 2) + pair] = rows.T.astype(bf16)

    def prepare_own(i, carry):
        for x in range(4):
            for pair in range(1, EY // 2 - 1):
                prepare(x + 2, pair)
        return carry

    def prepare_sides(i, carry):
        for x in range(4):
            for pair in (0, EY // 2 - 1):
                prepare(x + 2, pair)
        return carry

    def prepare_ends(i, carry):
        for x in range(2):
            for pair in range(EY // 2):
                prepare(i * (BX + 2) + x, pair)
        return carry

    def neighbour(b, k):
        code = codes[b, k]
        along = ((code * 13) >> 6) - 2
        across = code - (along + 2) * 5 - 2
        inside_x = gx * BX + b // BY + along
        inside_y = gy * BY + b % BY + across
        inside = (
            (inside_x >= 0)
            & (inside_x < n_gx * BX)
            & (inside_y >= 0)
            & (inside_y < n_gy * BY)
        )
        return along, across, inside

    def weigh_tile(b, k, own, along, across, inside):
        place = (b // BY + 2 + along) * EY + b % BY + 2 + across
        odd = (place & 1).astype(f32)
        shift = jnp.where(
            row8 == 0, along.astype(f32), jnp.where(row8 == 1, across.astype(f32), 0.0)
        )
        there = own - shift
        norm = -SHARPNESS * jnp.sum(there * there, axis=0, keepdims=True)
        norm = norm + jnp.where(inside, 0.0, FAR)
        rows = jnp.where(row8 == 3, norm, jnp.where(row8 == 4, 1.0, there * (2.0 * SHARPNESS)))
        p1, p2, p3 = split3(rows)
        rows = jnp.concatenate(
            [p1, p1, p2, p2, p1, p3, jnp.zeros((16, 256), f32)], axis=0
        ).astype(bf16)
        rows = jnp.concatenate(
            [rows * (1.0 - odd).astype(bf16), rows * odd.astype(bf16)], axis=0
        )
        tile = jnp.exp2(jnp.dot(points[place >> 1], rows, preferred_element_type=f32))
        tiles[b * NBR + k] = tile.astype(bf16)
        return jnp.sum(tile.reshape(32, 8, 256), axis=0)

    def weigh_self(i, carry):
        for c in range(8):
            b = i * 8 + c
            own = jnp.concatenate([pos[b // BY, b % BY], none], axis=0)
            still = jnp.int32(0)
            totals[b] = weigh_tile(b, 0, own, still, still, True)
        return carry

    def weigh(i, carry):
        for c in range(2):
            b = i * 2 + c
            own = jnp.concatenate([pos[b // BY, b % BY], none], axis=0)
            total = totals[b]
            for k in range(1, NBR):
                total = total + weigh_tile(b, k, own, *neighbour(b, k))
            totals[b] = total
        for half, after in enumerate(PASS_AFTER):

            @pl.when(i == after)
            def _():
                pass_load(half)

        return carry

    prepare_own(0, 0)
    lax.fori_loop(0, 2, weigh_self, 0)
    for copy in pos_copies:
        copy.wait_recv()
    prepare_sides(0, 0)
    lax.fori_loop(0, 2, prepare_ends, 0)

    lax.fori_loop(0, BINS // 2, weigh, 0)

    def mix(framed, b):
        sources = []
        for k in range(NBR):
            along, across, _ = neighbour(b, k)
            sources.append(framed[b // BY + 2 + along, b % BY + 2 + across])
        sources = jnp.concatenate(sources, axis=1)
        weights = tiles[pl.ds(b * NBR, NBR)].reshape(NBR * 256, 256)
        mixture = jnp.dot(sources, weights, preferred_element_type=f32)
        mixture = mixture / jnp.sum(totals[b], axis=0, keepdims=True)
        speed = speeds[b]
        u = mixture[:32]
        v = mixture[32:]
        reacted = speed * u * v / (1.0 + speed * (u + v))
        return jnp.concatenate([u - reacted, v - reacted], axis=0).astype(bf16)

    own_load.wait()
    for half in range(2):
        for copy in load_along(half) + load_corners(half):
            copy.wait_recv()

    def row_at(i):
        return i + parity * (BX - 1 - 2 * i)

    def remote(kind, i, row, col, cols, to_row, to_col, sx, sy):
        return pltpu.make_async_remote_copy(
            src_ref=second.at[row, pl.ds(col, cols)],
            dst_ref=second.at[to_row, pl.ds(to_col, cols)],
            send_sem=halo_send.at[kind, i],
            recv_sem=halo_recv.at[kind, i],
            device_id=at(sx, sy),
            device_id_type=MESH,
        )

    def sides(i):
        row = row_at(i) + 2
        return [
            remote(0, i, row, 2, 2, row, BY + 2, 0, -1),
            remote(1, i, row, BY, 2, row, 0, 0, 1),
        ]

    def along(i, kinds):
        row = row_at(i) + 2
        dx = (row_at(i) // 2) * 2 - 1
        spans = {2: (2, BY), 3: (0, 2), 4: (BY + 2, 2)}
        return [
            remote(kind, i, row, *spans[kind], row - BX * dx, spans[kind][0], dx, 0)
            for kind in kinds
        ]

    def pass_on(i):
        for copy in sides(i):
            copy.wait_recv()
        for copy in along(i, (3, 4)):
            copy.start()

    def mix_row(i, carry):
        for j in range(BY):
            second[row_at(i) + 2, j + 2] = mix(first, row_at(i) * BY + j)
        for copy in sides(i) + along(i, (2,)):
            copy.start()

        @pl.when(i >= BX // 2)
        def _():
            pass_on(i - BX // 2)

        return carry

    lax.fori_loop(0, BX, mix_row, 0)
    for i in range(BX // 2, BX):
        pass_on(i)
    for i in range(BX):
        for copy in along(i, (2, 3, 4)):
            copy.wait_recv()

    def give(p):
        to = target(p)
        return pltpu.make_async_remote_copy(
            src_ref=packed.at[pl.ds(2 * p, 2)],
            dst_ref=out.at[pl.ds(2 * gy, 2)],
            send_sem=hand_send.at[p],
            recv_sem=hand_recv.at[p],
            device_id=(gx, to),
            device_id_type=MESH,
        )

    def pack(p):
        for c in range(2):
            keep = (amount[p] > c).astype(f32).astype(bf16)
            packed[2 * p + c] = final[jnp.minimum(begin[p] + c, BINS - 1)] * keep

    def step_two(i, carry):
        for c in range(2):
            final[2 * i + c] = mix(second, order[2 * i + c])
        pack(i)
        give(i).start()
        return carry

    lax.fori_loop(0, BINS // 2, step_two, 0)

    def rest(p, carry):
        pack(p)
        give(p).start()
        return carry

    lax.fori_loop(BINS // 2, n_gy - 1, rest, 0)
    pack(n_gy - 1)
    stay = pltpu.make_async_copy(
        packed.at[pl.ds(2 * n_gy - 2, 2)], out.at[pl.ds(2 * gy, 2)], own_sem.at[1]
    )
    stay.start()

    for copy in pos_copies:
        copy.wait_send()
    for half in range(2):
        for copy in load_sides(half) + load_along(half) + load_corners(half):
            copy.wait_send()
    for i in range(BX):
        for copy in sides(i) + along(i, (2, 3, 4)):
            copy.wait_send()

    def taken(p, carry):
        give(p).wait()
        return carry

    lax.fori_loop(0, n_gy - 1, taken, 0)
    stay.wait()


def body(n_gx, n_gy, load, pos, kelvin, factor, onset, codes, zone):
    species, walkers = load.shape[1:]
    anywhere = pl.BlockSpec(memory_space=pl.ANY)
    dma = pltpu.SemaphoreType.DMA
    return pl.pallas_call(
        functools.partial(kernel, n_gx, n_gy),
        out_shape=pltpu.VMEM((2 * n_gy, species, walkers), bf16),
        in_specs=[anywhere] * 7,
        out_specs=pl.BlockSpec(memory_space=pltpu.VMEM),
        scratch_shapes=[
            pltpu.SMEM((BINS, NBR), jnp.int32),
            pltpu.SMEM((1, BINS), jnp.int32),
            pltpu.VMEM((3, BINS, walkers), f32),
            pltpu.VMEM((BINS, walkers), f32),
            pltpu.VMEM((1, species // 2), f32),
            pltpu.VMEM((1, species // 2), f32),
            pltpu.VMEM((BX, BY, 3, walkers), f32),
            pltpu.VMEM((EX, EY, 3, walkers), f32),
            pltpu.VMEM((EX * EY // 2, walkers, 128), bf16),
            pltpu.VMEM((BINS * NBR, walkers, walkers), bf16),
            pltpu.VMEM((BINS, 8, walkers), f32),
            pltpu.VMEM((BINS, species // 2, walkers), f32),
            pltpu.VMEM((EX, EY, species, walkers), bf16),
            pltpu.VMEM((EX, EY, species, walkers), bf16),
            pltpu.VMEM((BINS, species, walkers), bf16),
            pltpu.VMEM((2 * n_gy, species, walkers), bf16),
            pltpu.SMEM((n_gy,), jnp.int32),
            pltpu.SMEM((BINS,), jnp.int32),
            pltpu.SMEM((n_gy,), jnp.int32),
            pltpu.SMEM((n_gy,), jnp.int32),
            dma((8,)),
            dma((8,)),
            dma((8,)),
            dma((5, 2)),
            dma((5, 2)),
            dma((5, BX)),
            dma((5, BX)),
            dma((n_gy,)),
            dma((n_gy,)),
        ],
        compiler_params=pltpu.CompilerParams(
            collective_id=0, has_side_effects=True, vmem_limit_bytes=56 * 1024 * 1024
        ),
    )(
        codes,
        zone.reshape(1, -1),
        pos.transpose(1, 0, 2),
        kelvin,
        factor.reshape(1, -1),
        onset.reshape(1, -1),
        load.reshape(BX, BY, species, walkers),
    )


def solution(mesh):
    both = ("gx", "gy")
    in_specs = (
        P(both, None, None),
        P(both, None, None),
        P(both, None),
        P(),
        P(),
        P(both, None),
        P(both, None),
    )
    return jax.shard_map(
        functools.partial(body, mesh.shape["gx"], mesh.shape["gy"]),
        mesh=mesh,
        in_specs=in_specs,
        out_specs=P(both, None, None),
        check_vma=False,
    )
```
